32 devices in a mesh: dp: 4 (over z), ctx: 8 (over y, x, core).
Axes of the slice: x: 2, y: 2, z: 4, core: 2. Of those that a mesh axis runs over, the one named last changes fastest.
Arguments:
- inputs: bfloat16 [4, 2048, 4096], P('dp', 'ctx'), may hold values from -6 to 6
- value_weight: bfloat16 [4096, 512], P('ctx'), may hold values from -0.09375 to 0.09375
- query_states: bfloat16 [4, 2048, 2048], P('dp', 'ctx'), may hold values from -40 to 40
- key_states: bfloat16 [4, 2048, 512], P('dp', 'ctx'), may hold values from -6 to 6
- value_states: bfloat16 [4, 2048, 512], P('dp', 'ctx'), may hold values from -6 to 6
- attention_out: bfloat16 [4, 2048, 2048], P('dp', 'ctx'), may hold values from -4 to 4
- out_grad: bfloat16 [4, 2048, 2048], P('dp', 'ctx'), may hold values from -6 to 6
- segment_ids: int32 [4, 2048], P('dp', 'ctx'), may hold values from 0 to 3, never falling along the last dimension, each value on 1 to 1024 neighbouring positions
Outputs:
- query_grad: bfloat16 [4, 2048, 2048], P('dp', 'ctx')
- key_grad: bfloat16 [4, 2048, 512], P('dp', 'ctx')
- input_grad: bfloat16 [4, 2048, 4096], P('dp', 'ctx')
- weight_grad: float32 [4096, 512], P('ctx')
The draws below stay inside these ranges and needn't reach their ends.
Inputs may be any that keep to these rules, and one draw needn't show every extreme that they name: `segment_ids`: along each sequence the ids never fall; each record holds 1 to 1024 tokens and one holds exactly 1024.
All inputs are finite; a program needn't handle non-finite values.
Results may differ from the reference program's by a relative error of at most 0.0057.
Values may be sent and summed in bfloat16 or wider, within the bound.
No kernel may reach another device: no remote copies, remote signals or barrier semaphores. Data moves between devices by JAX's collectives and lax.ppermute only.
A program may use at most 128 MiB of HBM per device.

```python
import math
import jax
import jax.numpy as jnp
import numpy as np
from jax import lax

D = 4096
HQ = 16
KVH = 4
DH = 128
W = 2048
TOK_DEV = 256
SPAN = 8
TOKENS = 2048
SEQS = 4
RECORDS = 4
MOST = 1024


def shared_draw(key):
    shape_kv = (SEQS, TOKENS, KVH, DH)
    drawn_rows = jax.random.truncated_normal(jax.random.fold_in(key, 11), -6.0, 6.0, shape_kv, jnp.float32)
    return drawn_rows


def draw_key_states(key, part):
    drawn_rows = shared_draw(key)
    return drawn_rows.reshape(SEQS, TOKENS, KVH * DH).astype(jnp.bfloat16)


def draw_query_states(key, part):
    group_size = HQ // KVH
    shape_q = (SEQS, TOKENS, KVH, group_size, DH)
    own_rows = jax.random.truncated_normal(jax.random.fold_in(key, 21), -6.0, 6.0, shape_q, jnp.float32)
    return own_rows.reshape(SEQS, TOKENS, HQ * DH).astype(jnp.bfloat16)


def raised(entries, rng, source, target, parts, factor):
    def block_of(axis_at):
        return (jnp.arange(entries.shape[axis_at]) // (entries.shape[axis_at] // parts)).reshape((-1,) + (1,) * (entries.ndim - 1 - axis_at))

    one_side = jax.random.permutation(rng, parts)[block_of(target)]
    far = (block_of(target) + parts // 2) % parts
    return jnp.where((block_of(source) == one_side) | (block_of(source) == far), factor * entries, entries)


def levels(own_key, shape, shards, smallest, top_value):
    level = 1.0
    for axis_at, parts in shards:
        heights = jax.random.uniform(jax.random.fold_in(jax.random.fold_in(own_key, 6), axis_at), (parts,), jnp.float32, smallest / len(shards), top_value / len(shards))
        level = level * jnp.repeat(jnp.exp(heights), shape[axis_at] // parts).reshape((-1,) + (1,) * (len(shape) - 1 - axis_at))
    return level


def profile(count, total, reach, slope):
    portions = [(1 << 20) // math.isqrt(grade ** slope) + 1 for grade in range(2, count + 1)]
    spare, given = total - reach - (count - 1), [1] * (count - 1)
    while spare > 0:
        movable = [i for i in range(count - 1) if given[i] < reach]
        pool, remaining = sum([portions[i] for i in movable]), spare
        for i in movable:
            addition = min(reach - given[i], max(1, remaining * portions[i] // pool), spare)
            given[i] = given[i] + addition
            spare = spare - addition
    return np.array([reach] + given)


def ragged(own_key, number_of, total, bound, skew):
    if number_of == 2:
        one = jax.random.randint(own_key, (), max(1, total - bound), min(bound, total - 1) + 1)
        return jnp.stack([one, total - one])
    lengths = jnp.asarray(profile(number_of, total, bound, skew), jnp.int32)
    twos = (number_of - 1) // 2
    donor, taker = lengths[1:1 + 2 * twos:2], lengths[2:2 + 2 * twos:2]
    margin = jnp.minimum(donor - 1, bound - taker)
    passed = jax.random.randint(jax.random.fold_in(own_key, 1), (twos,), 0, 1 << 20) % (margin + 1)
    lengths = lengths.at[1:1 + 2 * twos:2].set(donor - passed).at[2:2 + 2 * twos:2].set(taker + passed)
    return lengths[jax.random.permutation(jax.random.fold_in(own_key, 2), number_of)]


def gaussian(key, dims, spread, bound, pieces=(), held_as=jnp.bfloat16):
    array = spread * jax.random.normal(key, dims, jnp.float32)
    if pieces:
        array = array * levels(key, dims, pieces, -0.22, 0.18)
    return jnp.clip(array, -bound, bound).astype(held_as)


def bell_draw_with(key, shape, scale, limit, pieces, heavy, held_as=jnp.bfloat16):
    array = scale * jax.random.normal(key, shape, jnp.float32)
    if pieces:
        array = array * levels(key, shape, pieces, -0.22, 0.18)
    return jnp.clip(raised(array, jax.random.fold_in(key, 3), *heavy), -limit, limit).astype(held_as)


def setup_inputs(seed: int = 0) -> dict:
    streams_of = jax.random.split(jax.random.key(seed), 9)
    inputs = bell_draw_with(streams_of[0], (SEQS, TOKENS, D), 1.0, 6.0, ((0, 4), (1, 8)), (1, 2, 8, 2.0))
    value_weight = gaussian(streams_of[1], (D, KVH * DH), D ** -0.5, 0.09375, ((0, 8),))
    query_states = draw_query_states(jax.random.fold_in(streams_of[8], 71), 0)
    key_states = draw_key_states(jax.random.fold_in(streams_of[8], 71), 0)
    value_states = gaussian(streams_of[4], (SEQS, TOKENS, KVH * DH), 1.0, 6.0, ((0, 4), (1, 8)))
    attention_out = gaussian(streams_of[5], (SEQS, TOKENS, HQ * DH), 0.5, 4.0, ((0, 4), (1, 8)))
    out_grad = gaussian(streams_of[6], (SEQS, TOKENS, HQ * DH), 1.0, 6.0, ((0, 4), (1, 8)))
    segment_ids = jax.vmap(lambda own: jnp.searchsorted(jnp.cumsum(ragged(own, RECORDS, TOKENS, MOST, 2)), jnp.arange(TOKENS), side="right"))(jax.random.split(streams_of[7], SEQS)).reshape((SEQS, TOKENS)).astype(jnp.int32)
    return dict(inputs=inputs, value_weight=value_weight, query_states=query_states, key_states=key_states, value_states=value_states, attention_out=attention_out, out_grad=out_grad, segment_ids=segment_ids)


def record_starts(segment_ids):
    length = segment_ids.shape[0]
    position = jnp.arange(length, dtype=jnp.int32)
    begins = jnp.concatenate([jnp.ones((1,), dtype=jnp.bool_), segment_ids[1:] != segment_ids[:-1]])
    return lax.cummax(jnp.where(begins, position, jnp.zeros_like(position)), axis=0)

def attend_block(query_rows, key_rows, value_rows, grad_rows, output_rows, live_mask):
    factor = 1.0 / math.sqrt(DH)
    scores = jnp.einsum('rhgd,khd->hgrk', query_rows, key_rows) * factor
    scores = jnp.where(live_mask[None, None], scores, -1e+30)
    row_max = lax.optimization_barrier(jnp.max(scores, axis=-1, keepdims=True))
    exp_score = jnp.exp(scores - row_max)
    prob_full = exp_score / lax.optimization_barrier(jnp.sum(exp_score, axis=-1, keepdims=True))
    prob_low = lax.optimization_barrier(prob_full.astype(jnp.bfloat16)).astype(jnp.float32)
    row_delta = lax.optimization_barrier(jnp.sum(grad_rows * output_rows, axis=-1))
    prob_grad = jnp.einsum('rhgd,khd->hgrk', grad_rows, value_rows)
    score_grad = prob_full * (prob_grad - jnp.transpose(row_delta, (1, 2, 0))[..., None])
    score_grad = lax.optimization_barrier(score_grad.astype(jnp.bfloat16)).astype(jnp.float32)
    query_part = jnp.einsum('hgrk,khd->rhgd', score_grad, key_rows) * factor
    key_part = jnp.einsum('hgrk,rhgd->khd', score_grad, query_rows) * factor
    value_part = jnp.einsum('hgrk,rhgd->khd', prob_low, grad_rows)
    return (query_part, key_part, value_part)

def one_sequence(inputs, value_weight, query_states, key_states, value_states, attention_out, out_grad, segment_ids):
    starts = record_starts(segment_ids)
    group_size = HQ // KVH
    width_kv = KVH * DH
    span_rows = SPAN * TOK_DEV
    window_rows = span_rows + TOK_DEV
    pad_zero = jnp.zeros((span_rows, width_kv), jnp.float32)
    key_pad = jnp.concatenate([pad_zero, key_states.astype(jnp.float32)], axis=0)
    value_pad = jnp.concatenate([pad_zero, value_states.astype(jnp.float32)], axis=0)

    def block_step(carry, block_index):
        key_acc, value_acc = carry
        first_row = (block_index * TOK_DEV).astype(jnp.int32)
        query_rows = lax.dynamic_slice_in_dim(query_states, first_row, TOK_DEV, 0).astype(jnp.float32)
        query_rows = query_rows.reshape(TOK_DEV, KVH, group_size, DH)
        grad_rows = lax.dynamic_slice_in_dim(out_grad, first_row, TOK_DEV, 0).astype(jnp.float32)
        grad_rows = grad_rows.reshape(TOK_DEV, KVH, group_size, DH)
        output_rows = lax.dynamic_slice_in_dim(attention_out, first_row, TOK_DEV, 0).astype(jnp.float32)
        output_rows = output_rows.reshape(TOK_DEV, KVH, group_size, DH)
        key_rows = lax.dynamic_slice_in_dim(key_pad, first_row, window_rows, 0).reshape(window_rows, KVH, DH)
        value_rows = lax.dynamic_slice_in_dim(value_pad, first_row, window_rows, 0).reshape(window_rows, KVH, DH)
        query_pos = first_row + jnp.arange(TOK_DEV, dtype=jnp.int32)
        key_pos = first_row - span_rows + jnp.arange(window_rows, dtype=jnp.int32)
        query_start = lax.dynamic_slice_in_dim(starts, first_row, TOK_DEV, 0)
        live_mask = (key_pos[None, :] >= query_start[:, None]) & (key_pos[None, :] <= query_pos[:, None]) & (key_pos[None, :] > query_pos[:, None] - W)
        query_part, key_part, value_part = attend_block(query_rows, key_rows, value_rows, grad_rows, output_rows, live_mask)
        key_old = lax.dynamic_slice_in_dim(key_acc, first_row, window_rows, 0)
        key_acc = lax.dynamic_update_slice_in_dim(key_acc, key_old + key_part.reshape(window_rows, width_kv), first_row, 0)
        value_old = lax.dynamic_slice_in_dim(value_acc, first_row, window_rows, 0)
        value_acc = lax.dynamic_update_slice_in_dim(value_acc, value_old + value_part.reshape(window_rows, width_kv), first_row, 0)
        return ((key_acc, value_acc), query_part.reshape(TOK_DEV, HQ * DH).astype(jnp.bfloat16))
    zero_acc = jnp.zeros((TOKENS + span_rows, width_kv), jnp.float32)
    (key_acc, value_acc), query_grad = lax.scan(block_step, (zero_acc, zero_acc), jnp.arange(TOKENS // TOK_DEV, dtype=jnp.int32))
    query_grad = query_grad.reshape(TOKENS, HQ * DH)
    key_grad = key_acc[span_rows:].astype(jnp.bfloat16)
    value_delta = value_acc[span_rows:].astype(jnp.bfloat16)
    input_grad = jnp.dot(value_delta, value_weight.T, preferred_element_type=jnp.float32).astype(jnp.bfloat16)
    weight_part = jnp.dot(inputs.T, value_delta, preferred_element_type=jnp.float32)
    return (query_grad, key_grad, input_grad, weight_part)

def reference(inputs, value_weight, query_states, key_states, value_states, attention_out, out_grad, segment_ids):
    query_list = []
    key_list = []
    input_list = []
    weight_grad = jnp.zeros((D, KVH * DH), jnp.float32)
    for seq_index in range(SEQS):
        query_grad, key_grad, input_grad, weight_part = one_sequence(inputs[seq_index], value_weight, query_states[seq_index], key_states[seq_index], value_states[seq_index], attention_out[seq_index], out_grad[seq_index], segment_ids[seq_index])
        query_list.append(query_grad)
        key_list.append(key_grad)
        input_list.append(input_grad)
        weight_grad = weight_grad + weight_part
    return (jnp.stack(query_list), jnp.stack(key_list), jnp.stack(input_list), weight_grad)
```

```python
import functools
import math

import jax
import jax.numpy as jnp
from jax import lax
from jax.experimental import pallas as pl
from jax.experimental.pallas import tpu as pltpu
from jax.sharding import PartitionSpec as P

HQ = 16
KVH = 4
DH = 128
W = 2048
GROUP = HQ // KVH
NEG = -1e30
SEG_ROWS = 16
BF16 = jnp.bfloat16
F32 = jnp.float32


def nt_dot(a, b):
    return lax.dot_general(a, b, (((1,), (1,)), ((), ())), preferred_element_type=F32)


def nn_dot(a, b):
    return lax.dot_general(a, b, (((1,), (0,)), ((), ())), preferred_element_type=F32)


def tn_dot(a, b):
    return lax.dot_general(a, b, (((0,), (0,)), ((), ())), preferred_element_type=F32)


def attend_kernel(chips_back, tok, idx_ref, *refs):
    blocks = chips_back + 1
    slots = 2 * blocks
    q_ref, grad_ref, out_ref = refs[:3]
    same_refs = refs[3 : 3 + blocks]
    sib_refs = refs[3 + blocks : 3 + 2 * blocks]
    same_seg = refs[3 + 2 * blocks : 3 + 3 * blocks]
    sib_seg = refs[3 + 3 * blocks : 3 + 4 * blocks]
    dq_ref, same_out, sib_out = refs[3 + 4 * blocks : 6 + 4 * blocks]
    (win, key_t, q4, g4, exp_s, max_s, acc, dq_t, prob_s, ds_s, low_s, lo_s) = refs[
        6 + 4 * blocks :
    ]
    head = pl.program_id(0)
    here = idx_ref[0]
    core = lax.rem(here, 2)
    chip = lax.div(here, 2)
    base0 = 2 * (chip - chips_back) * tok
    own_slot = 2 * chips_back + core
    factor = 1.0 / math.sqrt(DH)
    scale = factor * math.log2(math.e)
    iota_k = lax.broadcasted_iota(jnp.int32, (tok, tok), 0)
    iota_q = lax.broadcasted_iota(jnp.int32, (tok, tok), 1)

    def slot_of(d, which):
        return 2 * (chips_back - d) + which

    @pl.when(head == 0)
    def _():
        mine = same_seg[0][0:1, 0:tok].astype(F32)
        count = jnp.zeros((1, tok), F32)
        for d in range(blocks):
            for which, seg in ((core, same_seg[d]), (1 - core, sib_seg[d])):
                row = seg[0:1, 0:tok].astype(F32)
                column = jnp.broadcast_to(row, (tok, tok)).T
                below = jnp.sum(jnp.where(column < mine, 1.0, 0.0), axis=0, keepdims=True)
                valid = (chip >= d).astype(F32)
                count = count + below * valid
        start = count.astype(jnp.int32) + jnp.maximum(base0, 0)
        query_pos = here * tok + lax.broadcasted_iota(jnp.int32, (1, tok), 1)
        low = jnp.maximum(start, query_pos - (W - 1))
        low_s[...] = jnp.broadcast_to(low, low_s.shape)
        lo_s[0] = lax.div(jnp.min(low.astype(F32)).astype(jnp.int32) - base0, tok)

    for d in range(blocks):
        for which, ref in ((core, same_refs[d]), (1 - core, sib_refs[d])):
            slot = slot_of(d, which)
            win[slot] = ref[...]
            key_t[slot] = ref[0:tok, :].T
    acc[...] = jnp.zeros_like(acc)
    dq_t[...] = jnp.zeros_like(dq_t)
    deltas = []
    for h in range(GROUP):
        cols = slice(h * DH, (h + 1) * DH)
        rows = slice(h * tok, (h + 1) * tok)
        q4[rows] = q_ref[:, cols]
        g4[rows] = grad_ref[:, cols]
        prod = grad_ref[:, cols].astype(F32) * out_ref[:, cols].astype(F32)
        deltas.append(jnp.sum(prod.T, axis=0, keepdims=True))
    low = low_s[0:1]

    def first(t, carry, diagonal):
        keys = win[t, 0:tok]
        bound = low - (base0 + t * tok)
        keep = iota_k >= bound
        if diagonal:
            keep = keep & (iota_k <= iota_q)
        maxes, sums = carry
        new_maxes, new_sums = [], []
        for h in range(GROUP):
            rows = slice(h * tok, (h + 1) * tok)
            s = jnp.where(keep, nt_dot(keys, q4[rows]), NEG)
            m = jnp.maximum(maxes[h], jnp.max(s, axis=0, keepdims=True))
            e = jnp.exp2((s - m) * scale)
            exp_s[t, :, rows] = e
            max_s[t, h : h + 1] = m
            new_maxes.append(m)
            new_sums.append(
                sums[h] * jnp.exp2((maxes[h] - m) * scale) + jnp.sum(e, axis=0, keepdims=True)
            )
        return tuple(new_maxes), tuple(new_sums)

    lo = lo_s[0]
    empty = (
        tuple(jnp.full((1, tok), NEG, F32) for _ in range(GROUP)),
        tuple(jnp.zeros((1, tok), F32) for _ in range(GROUP)),
    )
    stats = lax.fori_loop(lo, own_slot, lambda t, c: first(t, c, False), empty)
    maxes, sums = first(own_slot, stats, True)
    inverse = [1.0 / total for total in sums]

    def second(t, carry):
        values = win[t, tok : 2 * tok]
        for h in range(GROUP):
            rows = slice(h * tok, (h + 1) * tok)
            weight = jnp.exp2((max_s[t, h : h + 1] - maxes[h]) * scale) * inverse[h]
            prob = exp_s[t, :, rows] * weight
            prob_grad = nt_dot(values, g4[rows])
            ds_s[:, rows] = (prob * (prob_grad - deltas[h])).astype(BF16)
            prob_s[:, rows] = prob.astype(BF16)
        acc[t, tok : 2 * tok] = nn_dot(prob_s[...], g4[...])
        acc[t, 0:tok] = nn_dot(ds_s[...], q4[...]) * factor
        dq_t[...] += nn_dot(key_t[t], ds_s[...])
        return carry

    lax.fori_loop(lo, own_slot + 1, second, 0)
    for h in range(GROUP):
        rows = slice(h * tok, (h + 1) * tok)
        dq_ref[:, h * DH : (h + 1) * DH] = (dq_t[:, rows].T * factor).astype(BF16)
    for d in range(blocks):
        same_out[d] = acc[slot_of(d, core)]
        sib_out[d] = acc[slot_of(d, 1 - core)].astype(BF16)


def attend(index, query, grad, output, same, sibling):
    tok = query.shape[0]
    blocks = len(same)
    slots = 2 * blocks
    width = KVH * DH
    wide = GROUP * DH
    rows = GROUP * tok
    head_spec = pl.BlockSpec((tok, wide), lambda g, s: (0, g))
    kv_spec = pl.BlockSpec((2 * tok, DH), lambda g, s: (0, g))
    seg_spec = pl.BlockSpec((SEG_ROWS, width), lambda g, s: (2 * tok // SEG_ROWS, 0))
    part_spec = pl.BlockSpec((blocks, 2 * tok, DH), lambda g, s: (0, 0, g))
    pairs = tok * (blocks * 2 - 1) * tok * HQ
    return pl.pallas_call(
        functools.partial(attend_kernel, blocks - 1, tok),
        grid_spec=pltpu.PrefetchScalarGridSpec(
            num_scalar_prefetch=1,
            grid=(KVH,),
            in_specs=[head_spec] * 3 + [kv_spec] * slots + [seg_spec] * slots,
            out_specs=[head_spec, part_spec, part_spec],
            scratch_shapes=[
                pltpu.VMEM((slots, 2 * tok, DH), BF16),
                pltpu.VMEM((slots, DH, tok), BF16),
                pltpu.VMEM((rows, DH), BF16),
                pltpu.VMEM((rows, DH), BF16),
                pltpu.VMEM((slots, tok, rows), F32),
                pltpu.VMEM((slots, 8, tok), F32),
                pltpu.VMEM((slots, 2 * tok, DH), F32),
                pltpu.VMEM((DH, rows), F32),
                pltpu.VMEM((tok, rows), BF16),
                pltpu.VMEM((tok, rows), BF16),
                pltpu.VMEM((8, tok), jnp.int32),
                pltpu.SMEM((1,), jnp.int32),
            ],
        ),
        out_shape=[
            jax.ShapeDtypeStruct((tok, HQ * DH), BF16),
            jax.ShapeDtypeStruct((blocks, 2 * tok, width), F32),
            jax.ShapeDtypeStruct((blocks, 2 * tok, width), BF16),
        ],
        cost_estimate=pl.CostEstimate(
            flops=20 * pairs * DH, bytes_accessed=12 << 20, transcendentals=pairs
        ),
        name="attend",
    )(index, query, grad, output, *same, *sibling, *same, *sibling)


def weight_kernel(count, *refs):
    out_ref = refs[2 * count]
    for s in range(count):
        part = tn_dot(refs[s][...], refs[count + s][...])
        if s == 0:
            out_ref[...] = part
        else:
            out_ref[...] += part


def weight_product(rows, deltas):
    count = len(rows)
    tok, depth = rows[0].shape
    width = deltas[0].shape[1]
    return pl.pallas_call(
        functools.partial(weight_kernel, count),
        out_shape=jax.ShapeDtypeStruct((depth, width), F32),
        cost_estimate=pl.CostEstimate(
            flops=2 * count * tok * depth * width,
            bytes_accessed=count * tok * (depth + width) * 2 + depth * width * 4,
            transcendentals=0,
        ),
        name="weight_product",
    )(*rows, *deltas)


def shifted(block, axis, distance):
    devices = range(lax.axis_size(axis))
    route = [(i, i + distance) for i in devices if i + distance in devices]
    return lax.ppermute(block, axis, route)


def swapped(block, axis, mask):
    return lax.ppermute(block, axis, [(i, i ^ mask) for i in range(lax.axis_size(axis))])


def gathered(block, axis):
    size = lax.axis_size(axis)
    even = [block if m == 0 else swapped(block, axis, m) for m in range(0, size, 2)]
    odd = swapped(jnp.stack(even), axis, 1)
    return [(even[m // 2] if m % 2 == 0 else odd[m // 2]) for m in range(size)]


def summed(part, axis):
    size = lax.axis_size(axis)
    here = lax.axis_index(axis)
    masks = []
    mask = 1
    while mask < size:
        masks.append(mask)
        mask *= 2
    for mask in masks[:-1]:
        half = part.shape[0] // 2
        bit = (here // mask) % 2
        keep = lax.dynamic_slice_in_dim(part, bit * half, half, 0)
        send = lax.dynamic_slice_in_dim(part, (1 - bit) * half, half, 0)
        part = keep + swapped(send.astype(BF16), axis, mask).astype(F32)
    if masks:
        low = part.astype(BF16)
        part = low.astype(F32) + swapped(low, axis, masks[-1]).astype(F32)
    for mask in reversed(masks[:-1]):
        low = part.astype(BF16)
        other = swapped(low, axis, mask)
        bit = (here // mask) % 2
        part = jnp.concatenate(
            [jnp.where(bit == 0, low, other), jnp.where(bit == 0, other, low)]
        ).astype(F32)
    return part


def input_kernel(count, idx_ref, delta_ref, *refs):
    out_ref = refs[count]
    delta = delta_ref[...]
    depth = refs[0].shape[0]
    for s in range(count):
        column = pl.multiple_of((idx_ref[0] ^ s) * depth, depth)
        out_ref[:, pl.ds(column, depth)] = nt_dot(delta, refs[s][...]).astype(BF16)


def input_product(index, delta, weights):
    count = len(weights)
    tok, width = delta.shape
    depth = weights[0].shape[0]
    if depth % 128:
        full = jnp.stack(weights)
        order = jnp.arange(count) ^ index[0]
        full = jnp.take(full, order, axis=0).reshape(count * depth, width)
        product = jnp.einsum("tk,rk->tr", delta, full, preferred_element_type=F32)
        return product.astype(BF16)
    vmem = pl.BlockSpec(memory_space=pltpu.VMEM)
    return pl.pallas_call(
        functools.partial(input_kernel, count),
        in_specs=[pl.BlockSpec(memory_space=pltpu.SMEM)] + [vmem] * (1 + count),
        out_specs=vmem,
        out_shape=jax.ShapeDtypeStruct((tok, count * depth), BF16),
        cost_estimate=pl.CostEstimate(
            flops=2 * count * tok * depth * width,
            bytes_accessed=count * depth * (width + tok) * 2,
            transcendentals=0,
        ),
        name="input_product",
    )(index, delta, *weights)


def on_device(
    inputs,
    value_weight,
    query_states,
    key_states,
    value_states,
    attention_out,
    out_grad,
    segment_ids,
):
    size = lax.axis_size("ctx")
    here = lax.axis_index("ctx")
    tok = query_states.shape[1]
    depth = value_weight.shape[0]
    width = KVH * DH
    index = here.astype(jnp.int32).reshape(1)
    reach = min(W, size * tok // 2)
    chips_back = -(-(-(-(reach - 1) // tok)) // 2)
    seg = jnp.pad(segment_ids.astype(BF16), ((0, SEG_ROWS - 1), (0, width - tok)))
    own = jnp.concatenate([key_states[0], value_states[0], seg], axis=0)
    same = [own] + [shifted(own, "ctx", 2 * d) for d in range(1, chips_back + 1)]
    sibling = [swapped(block, "ctx", 1) for block in same]
    query_grad, same_part, sib_part = attend(
        index, query_states[0], out_grad[0], attention_out[0], same, sibling
    )
    rows = [
        lax.dynamic_slice_in_dim(inputs[0], (here ^ m) * depth, depth, 1) for m in range(size)
    ]
    rows = [rows[0]] + [swapped(rows[m], "ctx", m) for m in range(1, size)]
    weights = gathered(value_weight, "ctx")

    part = swapped(sib_part, "ctx", 1)
    total = same_part[0] + part[0].astype(F32)
    for d in range(1, chips_back + 1):
        chip_sum = (same_part[d] + part[d].astype(F32)).astype(BF16)
        total = total + shifted(chip_sum, "ctx", -2 * d).astype(F32)
    low = total.astype(BF16)
    key_grad = low[:tok]
    value_delta = low[tok:]
    deltas = gathered(value_delta, "ctx")
    weight_grad = summed(weight_product(rows, deltas), "dp")
    input_grad = input_product(index, value_delta, weights)
    return (query_grad[None], key_grad[None], input_grad[None], weight_grad)


def solution(mesh):
    placed = (
        P("dp", "ctx", None),
        P("ctx", None),
        P("dp", "ctx", None),
        P("dp", "ctx", None),
        P("dp", "ctx", None),
        P("dp", "ctx", None),
        P("dp", "ctx", None),
        P("dp", "ctx"),
    )
    return jax.shard_map(
        on_device,
        mesh=mesh,
        in_specs=placed,
        out_specs=(
            P("dp", "ctx", None),
            P("dp", "ctx", None),
            P("dp", "ctx", None),
            P("ctx", None),
        ),
        check_vma=False,
    )
```

```python
import functools
import math

import jax
import jax.numpy as jnp
from jax import lax
from jax.experimental import pallas as pl
from jax.experimental.pallas import tpu as pltpu
from jax.sharding import PartitionSpec as P


HQ = 16
KVH = 4
DH = 128
W = 2048
GROUP = HQ // KVH
NEG = -1e30
SEG_ROWS = 16
BF16 = jnp.bfloat16
F32 = jnp.float32


def nt_dot(a, b):
    return lax.dot_general(a, b, (((1,), (1,)), ((), ())), preferred_element_type=F32)


def nn_dot(a, b):
    return lax.dot_general(a, b, (((1,), (0,)), ((), ())), preferred_element_type=F32)


def tn_dot(a, b):
    return lax.dot_general(a, b, (((0,), (0,)), ((), ())), preferred_element_type=F32)


def attend_kernel(blocks, distances, tok, idx_ref, *refs):
    chips_back = blocks - 1
    count = len(distances)
    q_ref, grad_ref, out_ref = refs[:3]
    same_refs = refs[3 : 3 + count]
    sib_refs = refs[3 + count : 3 + 2 * count]
    same_seg = refs[3 + 2 * count : 3 + 3 * count]
    sib_seg = refs[3 + 3 * count : 3 + 4 * count]
    dq_ref, same_out, sib_out = refs[3 + 4 * count : 6 + 4 * count]
    (win, key_t, q4, g4, exp_s, max_s, acc, dq_t, prob_s, ds_s, low_s, lo_s) = refs[
        6 + 4 * count :
    ]
    head = pl.program_id(0)
    here = idx_ref[0]
    core = lax.rem(here, 2)
    chip = lax.div(here, 2)
    base0 = 2 * (chip - chips_back) * tok
    own_slot = 2 * chips_back + core
    factor = 1.0 / math.sqrt(DH)
    scale = factor * math.log2(math.e)
    iota_k = lax.broadcasted_iota(jnp.int32, (tok, tok), 0)
    iota_q = lax.broadcasted_iota(jnp.int32, (tok, tok), 1)

    def slot_of(d, which):
        return 2 * (chips_back - d) + which

    @pl.when(head == 0)
    def _():
        mine = same_seg[0][0:1, 0:tok].astype(F32)
        total = jnp.zeros((1, tok), F32)
        for d, serves, *segs in zip(*zip(*distances), same_seg, sib_seg):
            valid = (serves(chip) & (chip >= d)).astype(F32)
            for seg in segs:
                row = seg[0:1, 0:tok].astype(F32)
                column = jnp.broadcast_to(row, (tok, tok)).T
                below = jnp.sum(jnp.where(column < mine, 1.0, 0.0), axis=0, keepdims=True)
                total = total + below * valid
        start = total.astype(jnp.int32) + jnp.maximum(base0, 0)
        query_pos = here * tok + lax.broadcasted_iota(jnp.int32, (1, tok), 1)
        low = jnp.maximum(start, query_pos - (W - 1))
        low_s[...] = jnp.broadcast_to(low, low_s.shape)
        lo_s[0] = lax.div(jnp.min(low.astype(F32)).astype(jnp.int32) - base0, tok)

    for d, serves, same_ref, sib_ref in zip(*zip(*distances), same_refs, sib_refs):

        @pl.when(serves(chip))
        def _(d=d, same_ref=same_ref, sib_ref=sib_ref):
            for which, ref in ((core, same_ref), (1 - core, sib_ref)):
                slot = slot_of(d, which)
                win[slot] = ref[...]
                key_t[slot] = ref[0:tok, :].T

    acc[...] = jnp.zeros_like(acc)
    dq_t[...] = jnp.zeros_like(dq_t)
    deltas = []
    for h in range(GROUP):
        cols = slice(h * DH, (h + 1) * DH)
        rows = slice(h * tok, (h + 1) * tok)
        q4[rows] = q_ref[:, cols]
        g4[rows] = grad_ref[:, cols]
        prod = grad_ref[:, cols].astype(F32) * out_ref[:, cols].astype(F32)
        deltas.append(jnp.sum(prod.T, axis=0, keepdims=True))
    low = low_s[0:1]

    def first(t, carry, diagonal):
        keys = win[t, 0:tok]
        bound = low - (base0 + t * tok)
        keep = iota_k >= bound
        if diagonal:
            keep = keep & (iota_k <= iota_q)
        maxes, sums = carry
        new_maxes, new_sums = [], []
        for h in range(GROUP):
            rows = slice(h * tok, (h + 1) * tok)
            s = jnp.where(keep, nt_dot(keys, q4[rows]), NEG)
            m = jnp.maximum(maxes[h], jnp.max(s, axis=0, keepdims=True))
            e = jnp.exp2((s - m) * scale)
            exp_s[t, :, rows] = e
            max_s[t, h : h + 1] = m
            new_maxes.append(m)
            new_sums.append(
                sums[h] * jnp.exp2((maxes[h] - m) * scale) + jnp.sum(e, axis=0, keepdims=True)
            )
        return tuple(new_maxes), tuple(new_sums)

    lo = lo_s[0]
    empty = (
        tuple(jnp.full((1, tok), NEG, F32) for _ in range(GROUP)),
        tuple(jnp.zeros((1, tok), F32) for _ in range(GROUP)),
    )
    stats = lax.fori_loop(lo, own_slot, lambda t, c: first(t, c, False), empty)
    maxes, sums = first(own_slot, stats, True)
    inverse = [1.0 / total for total in sums]

    def second(t, carry):
        values = win[t, tok : 2 * tok]
        for h in range(GROUP):
            rows = slice(h * tok, (h + 1) * tok)
            weight = jnp.exp2((max_s[t, h : h + 1] - maxes[h]) * scale) * inverse[h]
            prob = exp_s[t, :, rows] * weight
            prob_grad = nt_dot(values, g4[rows])
            ds_s[:, rows] = (prob * (prob_grad - deltas[h])).astype(BF16)
            prob_s[:, rows] = prob.astype(BF16)
        acc[t, tok : 2 * tok] = nn_dot(prob_s[...], g4[...])
        acc[t, 0:tok] = nn_dot(ds_s[...], q4[...]) * factor
        dq_t[...] += nn_dot(key_t[t], ds_s[...])
        return carry

    lax.fori_loop(lo, own_slot + 1, second, 0)
    for h in range(GROUP):
        rows = slice(h * tok, (h + 1) * tok)
        dq_ref[:, h * DH : (h + 1) * DH] = (dq_t[:, rows].T * factor).astype(BF16)
    for d in range(blocks):
        same_out[d] = acc[slot_of(d, core)]
        sib_out[d] = acc[slot_of(d, 1 - core)].astype(BF16)


def attend(index, query, grad, output, distances, same, sibling):
    tok = query.shape[0]
    blocks = 1 + max(d for d, _ in distances)
    slots = 2 * blocks
    count = len(same) + len(sibling)
    width = KVH * DH
    wide = GROUP * DH
    rows = GROUP * tok
    head_spec = pl.BlockSpec((tok, wide), lambda g, s: (0, g))
    kv_spec = pl.BlockSpec((2 * tok, DH), lambda g, s: (0, g))
    seg_spec = pl.BlockSpec((SEG_ROWS, width), lambda g, s: (2 * tok // SEG_ROWS, 0))
    part_spec = pl.BlockSpec((blocks, 2 * tok, DH), lambda g, s: (0, 0, g))
    pairs = tok * (blocks * 2 - 1) * tok * HQ
    return pl.pallas_call(
        functools.partial(attend_kernel, blocks, distances, tok),
        grid_spec=pltpu.PrefetchScalarGridSpec(
            num_scalar_prefetch=1,
            grid=(KVH,),
            in_specs=[head_spec] * 3 + [kv_spec] * count + [seg_spec] * count,
            out_specs=[head_spec, part_spec, part_spec],
            scratch_shapes=[
                pltpu.VMEM((slots, 2 * tok, DH), BF16),
                pltpu.VMEM((slots, DH, tok), BF16),
                pltpu.VMEM((rows, DH), BF16),
                pltpu.VMEM((rows, DH), BF16),
                pltpu.VMEM((slots, tok, rows), F32),
                pltpu.VMEM((slots, 8, tok), F32),
                pltpu.VMEM((slots, 2 * tok, DH), F32),
                pltpu.VMEM((DH, rows), F32),
                pltpu.VMEM((tok, rows), BF16),
                pltpu.VMEM((tok, rows), BF16),
                pltpu.VMEM((8, tok), jnp.int32),
                pltpu.SMEM((1,), jnp.int32),
            ],
        ),
        out_shape=[
            jax.ShapeDtypeStruct((tok, HQ * DH), BF16),
            jax.ShapeDtypeStruct((blocks, 2 * tok, width), F32),
            jax.ShapeDtypeStruct((blocks, 2 * tok, width), BF16),
        ],
        cost_estimate=pl.CostEstimate(
            flops=20 * pairs * DH, bytes_accessed=12 << 20, transcendentals=pairs
        ),
        name="attend",
    )(index, query, grad, output, *same, *sibling, *same, *sibling)


def weight_kernel(count, idx_ref, rows_ref, *refs):
    out_ref = refs[count]
    for s in range(count):
        part = tn_dot(rows_ref[idx_ref[0] ^ s], refs[s][...])
        if s == 0:
            out_ref[...] = part
        else:
            out_ref[...] += part


def weight_product(index, rows, deltas):
    count, tok, depth = rows.shape
    width = deltas[0].shape[1]
    vmem = pl.BlockSpec(memory_space=pltpu.VMEM)
    return pl.pallas_call(
        functools.partial(weight_kernel, count),
        in_specs=[pl.BlockSpec(memory_space=pltpu.SMEM)] + [vmem] * (1 + count),
        out_specs=vmem,
        out_shape=jax.ShapeDtypeStruct((depth, width), F32),
        cost_estimate=pl.CostEstimate(
            flops=2 * count * tok * depth * width,
            bytes_accessed=count * tok * (depth + width) * 2 + depth * width * 4,
            transcendentals=0,
        ),
        name="weight_product",
    )(index, rows, *deltas)


def split_kernel(in_ref, out_ref):
    out_ref[0] = in_ref[...]


def split_columns(block, count):
    rows, columns = block.shape
    depth = columns // count
    if depth % 128:
        return block.reshape(rows, count, depth).transpose(1, 0, 2)
    return pl.pallas_call(
        split_kernel,
        grid=(count,),
        in_specs=[pl.BlockSpec((rows, depth), lambda j: (0, j))],
        out_specs=pl.BlockSpec((1, rows, depth), lambda j: (j, 0, 0)),
        out_shape=jax.ShapeDtypeStruct((count, rows, depth), block.dtype),
        cost_estimate=pl.CostEstimate(
            flops=0, bytes_accessed=4 * rows * columns, transcendentals=0
        ),
        name="split_columns",
    )(block)


def shifted(block, axis, distance):
    devices = range(lax.axis_size(axis))
    route = [(i, i + distance) for i in devices if i + distance in devices]
    return lax.ppermute(block, axis, route)


def behind(own, axis, chips_back):
    def everyone(chip):
        return chip >= 0

    size = lax.axis_size(axis)
    here = lax.axis_index(axis)
    if size == 8 and chips_back == 2:
        over_y = lax.ppermute(own, axis, [(i, i + 4) for i in range(4)])
        over_x = lax.ppermute(own, axis, [(0, 2), (1, 3), (4, 6), (5, 7), (3, 1)])
        handed = lax.ppermute(jnp.where(here >= 4, over_y, over_x), axis, [(6, 4), (1, 5)])
        return [own, over_y, over_x, handed], (
            (0, everyone),
            (2, everyone),
            (1, lambda chip: chip != 2),
            (1, lambda chip: chip == 2),
        )
    same, distances = [own], [(0, everyone)]
    for d in range(1, chips_back + 1):
        same.append(shifted(own, axis, 2 * d))
        distances.append((d, everyone))
    return same, tuple(distances)


def swapped(block, axis, mask):
    return lax.ppermute(block, axis, [(i, i ^ mask) for i in range(lax.axis_size(axis))])


def gathered(block, axis):
    size = lax.axis_size(axis)
    even = [block]
    for m in range(2, size, 2):
        even.append(swapped(block, axis, m))
    blocks = []
    for block in even:
        blocks += [block, swapped(block, axis, 1)]
    return blocks


def summed(part, axis):
    size = lax.axis_size(axis)
    here = lax.axis_index(axis)
    masks = []
    mask = 1
    while mask < size:
        masks.append(mask)
        mask *= 2
    for mask in masks[:-1]:
        half = part.shape[0] // 2
        bit = (here // mask) % 2
        keep = lax.dynamic_slice_in_dim(part, bit * half, half, 0)
        send = lax.dynamic_slice_in_dim(part, (1 - bit) * half, half, 0)
        part = keep + swapped(send.astype(BF16), axis, mask).astype(F32)
    if masks:
        low = part.astype(BF16)
        other = swapped(low, axis, masks[-1])
        part = low.astype(F32) + other.astype(F32)
    for mask in reversed(masks[:-1]):
        low = part.astype(BF16)
        other = swapped(low, axis, mask)
        bit = (here // mask) % 2
        part = jnp.concatenate(
            [jnp.where(bit == 0, low, other), jnp.where(bit == 0, other, low)]
        ).astype(F32)
    return part


def input_kernel(count, idx_ref, delta_ref, *refs):
    out_ref = refs[count]
    delta = delta_ref[...]
    depth = refs[0].shape[0]
    for s in range(count):
        column = pl.multiple_of((idx_ref[0] ^ s) * depth, depth)
        out_ref[:, pl.ds(column, depth)] = nt_dot(delta, refs[s][...]).astype(BF16)


def input_product(index, delta, weights):
    count = len(weights)
    tok, width = delta.shape
    depth = weights[0].shape[0]
    if depth % 128:
        full = jnp.stack(weights)
        order = jnp.arange(count) ^ index[0]
        full = jnp.take(full, order, axis=0).reshape(count * depth, width)
        product = jnp.einsum("tk,rk->tr", delta, full, preferred_element_type=F32)
        return product.astype(BF16)
    vmem = pl.BlockSpec(memory_space=pltpu.VMEM)
    return pl.pallas_call(
        functools.partial(input_kernel, count),
        in_specs=[pl.BlockSpec(memory_space=pltpu.SMEM)] + [vmem] * (1 + count),
        out_specs=vmem,
        out_shape=jax.ShapeDtypeStruct((tok, count * depth), BF16),
        cost_estimate=pl.CostEstimate(
            flops=2 * count * tok * depth * width,
            bytes_accessed=count * depth * (width + tok) * 2,
            transcendentals=0,
        ),
        name="input_product",
    )(index, delta, *weights)


def on_device(
    inputs,
    value_weight,
    query_states,
    key_states,
    value_states,
    attention_out,
    out_grad,
    segment_ids,
):
    size = lax.axis_size("ctx")
    here = lax.axis_index("ctx")
    tok = query_states.shape[1]
    width = KVH * DH
    index = here.astype(jnp.int32).reshape(1)
    reach = min(W, size * tok // 2)
    chips_back = -(-(-(-(reach - 1) // tok)) // 2)
    seg = jnp.pad(segment_ids.astype(BF16), ((0, SEG_ROWS - 1), (0, width - tok)))
    own = jnp.concatenate([key_states[0], value_states[0], seg], axis=0)
    same, distances = behind(own, "ctx", chips_back)
    sibling = [swapped(block, "ctx", 1) for block in same]
    query_grad, same_part, sib_part = attend(
        index, query_states[0], out_grad[0], attention_out[0], distances, same, sibling
    )
    rows = split_columns(inputs[0], size)
    rows = lax.all_to_all(rows, "ctx", 0, 0, tiled=True)
    weights = gathered(value_weight, "ctx")

    part = swapped(sib_part, "ctx", 1)
    total = same_part[0] + part[0].astype(F32)
    for d in range(1, chips_back + 1):
        chip_sum = (same_part[d] + part[d].astype(F32)).astype(BF16)
        total = total + shifted(chip_sum, "ctx", -2 * d).astype(F32)
    low = total.astype(BF16)
    key_grad = low[:tok]
    value_delta = low[tok:]
    deltas = gathered(value_delta, "ctx")
    weight_part = weight_product(index, rows, deltas)
    weight_grad = summed(weight_part, "dp")
    input_grad = input_product(index, value_delta, weights)
    return (query_grad[None], key_grad[None], input_grad[None], weight_grad)


def solution(mesh):
    placed = (
        P("dp", "ctx", None),
        P("ctx", None),
        P("dp", "ctx", None),
        P("dp", "ctx", None),
        P("dp", "ctx", None),
        P("dp", "ctx", None),
        P("dp", "ctx", None),
        P("dp", "ctx"),
    )
    return jax.shard_map(
        on_device,
        mesh=mesh,
        in_specs=placed,
        out_specs=(
            P("dp", "ctx", None),
            P("dp", "ctx", None),
            P("dp", "ctx", None),
            P("ctx", None),
        ),
        check_vma=False,
    )
```
